32 devices in a mesh: dp: 4 (over y, x), tensor: 8 (over z, core).
Axes of the slice: x: 2, y: 2, z: 4, core: 2. Of those that a mesh axis runs over, the one named last changes fastest.
Arguments:
- tokens: bfloat16 [8192, 1408], P(('dp', 'tensor')), may hold values from -6 to 6
- norm_gain: float32 [1408], replicated, may hold values from 0.1 to 1.9
- norm_bias: float32 [1408], replicated, may hold values from -3 to 3
- qkv_weight: bfloat16 [1408, 3, 1408], P(None, None, 'dp'), may hold values from -0.15625 to 0.15625
- qkv_bias: float32 [3, 1408], P(None, 'dp'), may hold values from -20 to 20
- out_weight: bfloat16 [1408, 1408], P('dp'), may hold values from -0.15625 to 0.15625
- out_bias: float32 [1408], replicated, may hold values from -3 to 3
- merger_weight: bfloat16 [5632, 2048], P(None, 'dp'), may hold values from -0.078125 to 0.078125
- image_grids: int32 [4, 8, 2], replicated, may hold values from 8 to 16, as said below
Outputs:
- projected: bfloat16 [2048, 2048], P(('dp', 'tensor'))
- image_rms: float32 [4, 8], P('dp')
- image_max: float32 [4, 8], P('dp')
The draws below stay inside these ranges and needn't reach their ends.
Inputs may be any that keep to these rules, and one draw needn't show every extreme that they name: `image_grids`: every side is even; every group has at least one image of 16 x 16 patches.
All inputs are finite; a program needn't handle non-finite values.
Results may differ from the reference program's by a relative error of at most 0.006.
The reference program's roundings to bfloat16 on the way count: a program that leaves them out, or rounds other values in their place, can miss the bound.
Values may be sent and summed in bfloat16 or wider, within the bound.
A program may use at most 64 MiB of HBM per device.

```python
import math
import jax
import jax.numpy as jnp
from jax import lax

D = 1408
HEADS = 16
HD = 88
PROJ = 2048
GRID = 16
GMIN = 8
TOK_DEV = 256
GROUPS = 4
IMG = 8
TOKENS = 8192
N_DP = 4
N_TENSOR = 8


def draw_image_grids(key, part):
    side_key, pick_key = jax.random.split(jax.random.fold_in(key, 11))
    sides = 2 * jax.random.randint(side_key, (GROUPS, IMG, 2), GMIN // 2, GRID // 2 + 1)
    chosen = jax.random.randint(pick_key, (GROUPS, 1, 1), 0, IMG)
    slots = jnp.arange(IMG, dtype=jnp.int32)[None, :, None]
    return jnp.where(slots == chosen, GRID, sides).astype(jnp.int32)


def draw_qkv_bias(key, part):
    base_key = jax.random.fold_in(jax.random.fold_in(key, 23), 0)
    base_values = 0.5 * jnp.clip(jax.random.normal(base_key, (3, D), jnp.float32), -3.0, 3.0)
    return base_values


def block_levels(stream_key, extent, cuts, low, high):
    factor_of = 1.0
    for axis_at, shards_of in cuts:
        steps = jax.random.uniform(jax.random.fold_in(jax.random.fold_in(stream_key, 6), axis_at), (shards_of,), jnp.float32, low / len(cuts), high / len(cuts))
        factor_of = factor_of * jnp.repeat(jnp.exp(steps), extent[axis_at] // shards_of).reshape((-1,) + (1,) * (len(extent) - 1 - axis_at))
    return factor_of


def gaussian(key, extent, scale, limit, cuts=(), held_as=jnp.bfloat16):
    entries = jax.random.normal(key, extent, jnp.float32) * scale
    if len(cuts) > 0:
        entries = block_levels(key, extent, cuts, -0.22, 0.18) * entries
    return jnp.clip(entries, min=-limit, max=limit).astype(held_as)


def setup_inputs(seed: int = 0) -> dict:
    splits = jax.random.split(jax.random.key(seed), 10)
    return {
        "tokens": gaussian(splits[0], (TOKENS, D), 1.0, 6.0, ((0, 32),)),
        "norm_gain": jnp.clip(1.0 + 0.18 * jax.random.normal(splits[1], (D,), jnp.float32), 0.1, 1.9),
        "norm_bias": gaussian(splits[2], (D,), 0.5, 3.0, (), jnp.float32),
        "qkv_weight": gaussian(splits[3], (D, 3, D), D ** -0.5, 0.15625, ((2, 4),)),
        "qkv_bias": draw_qkv_bias(jax.random.fold_in(splits[9], 71), 0),
        "out_weight": gaussian(splits[5], (D, D), D ** -0.5, 0.15625, ((0, 4),)),
        "out_bias": gaussian(splits[6], (D,), 0.5, 3.0, (), jnp.float32),
        "merger_weight": gaussian(splits[7], (4 * D, PROJ), (4 * D) ** -0.5, 0.078125, ((1, 4),)),
        "image_grids": draw_image_grids(jax.random.fold_in(splits[9], 71), 0),
    }


epsilon = 1e-06
floor_value = -1e+30

def layout(grid_table):
    heights = grid_table[:, 0]
    widths = grid_table[:, 1]
    lengths = heights * widths
    starts = jnp.cumsum(lengths) - lengths
    return (widths, lengths, starts)

def image_lookup(positions, starts, upper_limit):
    found = lax.optimization_barrier(jnp.sum((positions[:, None] >= starts[None, :]).astype(jnp.int32), axis=1)) - 1
    inside = (positions >= 0) & (positions < upper_limit)
    return jnp.where(inside, found, -1).astype(jnp.int32)

def merge_sources(merged_pos, widths, starts, sum_total):
    owner_image = image_lookup(merged_pos, starts // 4, sum_total // 4)
    clipped = jnp.maximum(owner_image, 0)
    selector = (clipped[:, None] == jnp.arange(widths.shape[0], dtype=jnp.int32)[None, :]).astype(jnp.int32)
    grid_width = lax.optimization_barrier(jnp.sum(selector * widths[None, :], axis=1))
    image_start = lax.optimization_barrier(jnp.sum(selector * starts[None, :], axis=1))
    offset = merged_pos - image_start // 4
    half_width = grid_width // 2
    grid_row = offset // half_width
    grid_col = offset - grid_row * half_width
    anchor = image_start + 2 * grid_row * grid_width + 2 * grid_col
    sources = jnp.stack([anchor, anchor + 1, anchor + grid_width, anchor + grid_width + 1], axis=1)
    sources = jnp.where(owner_image[:, None] >= 0, sources, 4 * merged_pos[:, None])
    return (sources.astype(jnp.int32), owner_image)

def normalize(token_rows, gain_values, bias_values):
    floats = token_rows.astype(jnp.float32)
    average = lax.optimization_barrier(jnp.mean(floats, axis=1, keepdims=True))
    centred = floats - average
    variance = lax.optimization_barrier(jnp.mean(centred * centred, axis=1, keepdims=True))
    return (centred * lax.rsqrt(variance + epsilon) * gain_values + bias_values).astype(jnp.bfloat16)

def attend_heads(queries, key_rows, value_rows, query_image, key_image, head_size):
    query_count = queries.shape[0]
    key_count = key_rows.shape[0]
    head_count = queries.shape[1] // head_size
    query_heads = queries.reshape(query_count, head_count, head_size).astype(jnp.float32)
    key_heads = key_rows.reshape(key_count, head_count, head_size).astype(jnp.float32)
    value_heads = value_rows.reshape(key_count, head_count, head_size).astype(jnp.float32)
    allowed = (query_image[:, None] == key_image[None, :]) & (query_image[:, None] >= 0)
    scores = jnp.einsum('qhd,khd->hqk', query_heads, key_heads, precision=lax.Precision.HIGHEST) * (1.0 / math.sqrt(head_size))
    scores = jnp.where(allowed[None], scores, floor_value)
    largest = lax.optimization_barrier(jnp.max(scores, axis=2, keepdims=True))
    weights = jnp.exp(scores - largest) * allowed[None].astype(jnp.float32)
    denominator = lax.optimization_barrier(jnp.sum(weights, axis=2))
    denominator = jnp.where(query_image[None, :] >= 0, denominator, 1.0)
    rounded = lax.optimization_barrier(weights.astype(jnp.bfloat16)).astype(jnp.float32)
    summed = jnp.einsum('hqk,khd->qhd', rounded, value_heads, precision=lax.Precision.HIGHEST)
    summed = summed / jnp.transpose(denominator)[:, :, None]
    return summed.reshape(query_count, head_count * head_size)

def reference(tokens, norm_gain, norm_bias, qkv_weight, qkv_bias, out_weight, out_bias, merger_weight, image_grids):
    group_rows = TOK_DEV * N_TENSOR
    key_span = GRID * GRID
    block_size = min(TOK_DEV, 256)
    group_width = min(HEADS, 4) * HD
    quarter = group_rows // 4
    flat_weight = qkv_weight.reshape(D, 3 * D)
    flat_bias = qkv_bias.reshape(3 * D)
    projected_all = []
    rms_all = []
    peak_all = []
    for group in range(N_DP):
        token_rows = tokens[group * group_rows:(group + 1) * group_rows]
        widths, lengths, starts = layout(image_grids[group])
        sum_total = jnp.sum(lengths)
        own_image = image_lookup(jnp.arange(group_rows, dtype=jnp.int32), starts, sum_total)
        wide_image = image_lookup(jnp.arange(group_rows + 2 * key_span, dtype=jnp.int32) - key_span, starts, sum_total)
        normed = normalize(token_rows, norm_gain, norm_bias)
        qkv_rounded = (jnp.dot(normed, flat_weight, preferred_element_type=jnp.float32) + flat_bias).astype(jnp.bfloat16)
        qkv_rounded = lax.optimization_barrier(qkv_rounded)
        queries = qkv_rounded[:, :D]
        padding = jnp.zeros((key_span, 2 * D), jnp.bfloat16)
        padded_pairs = jnp.concatenate([padding, qkv_rounded[:, D:], padding], axis=0)

        def one_block(number):
            first_row = (number * block_size).astype(jnp.int32)
            query_part = lax.dynamic_slice_in_dim(queries, first_row, block_size, 0)
            pair_part = lax.dynamic_slice_in_dim(padded_pairs, first_row, block_size + 2 * key_span, 0)
            query_image = lax.dynamic_slice_in_dim(own_image, first_row, block_size, 0)
            key_image = lax.dynamic_slice_in_dim(wide_image, first_row, block_size + 2 * key_span, 0)
            pieces = []
            for column in range(0, D, group_width):
                pieces.append(attend_heads(query_part[:, column:column + group_width], pair_part[:, column:column + group_width], pair_part[:, D + column:D + column + group_width], query_image, key_image, HD))
            return jnp.concatenate(pieces, axis=1)
        attended = lax.map(one_block, jnp.arange(group_rows // block_size, dtype=jnp.int32))
        attended = attended.reshape(group_rows, D).astype(jnp.bfloat16)
        residual = token_rows.astype(jnp.float32) + jnp.dot(attended, out_weight, preferred_element_type=jnp.float32) + out_bias
        hidden = residual.astype(jnp.bfloat16)
        selector = (own_image[None, :] == jnp.arange(IMG, dtype=jnp.int32)[:, None]).astype(jnp.float32)
        square_sums = jnp.dot(selector, lax.optimization_barrier(jnp.sum(residual * residual, axis=1)), precision=lax.Precision.HIGHEST)
        rms_all.append(jnp.sqrt(square_sums / (lengths.astype(jnp.float32) * D)))
        sources, merged_image = merge_sources(jnp.arange(quarter, dtype=jnp.int32), widths, starts, sum_total)
        merged = jnp.take(hidden, sources.reshape(-1), axis=0).reshape(quarter, 4 * D)
        merged = jnp.where(merged_image[:, None] >= 0, merged, jnp.zeros((), jnp.bfloat16))
        projected = jnp.dot(merged, merger_weight, preferred_element_type=jnp.float32).astype(jnp.bfloat16)
        projected = lax.optimization_barrier(projected)
        row_peak = lax.optimization_barrier(jnp.max(projected.astype(jnp.float32), axis=1))
        matches = merged_image[None, :] == jnp.arange(IMG, dtype=jnp.int32)[:, None]
        peak_all.append(lax.optimization_barrier(jnp.max(jnp.where(matches, row_peak[None, :], floor_value), axis=1)))
        projected_all.append(projected)
    return (jnp.concatenate(projected_all, axis=0), jnp.stack(rms_all, axis=0), jnp.stack(peak_all, axis=0))
```

```python
import functools
import math

import jax
import jax.numpy as jnp
from jax import lax
from jax.experimental import pallas as pl
from jax.experimental.pallas import tpu as pltpu
from jax.sharding import PartitionSpec as P

HD = 88
GRID = 16
SPAN = GRID * GRID
EPS = 1e-06
FLOOR = -1e30
RATE = 1.0 / (math.sqrt(HD) * math.log(2.0))
MESH = pl.DeviceIdType.MESH
F32 = jnp.float32
BF16 = jnp.bfloat16


def kernel(
    nt,
    images,
    tokens_ref,
    gain_ref,
    nbias_ref,
    wqkv_hbm,
    bqkv_ref,
    ow_ref,
    obias_ref,
    mw_hbm,
    grids_ref,
    proj_ref,
    rms_ref,
    peak_ref,
    tok,
    normed,
    queries,
    kvx,
    att_out,
    att_in,
    owf,
    rim,
    merged,
    mw,
    pr_out,
    pr_in,
    squares_in,
    peaks_out,
    peaks_in,
    wqkv_ref,
    tok_sem,
    wq_sem,
    mw_sem,
    ow_sem,
    ag_sems,
    owg_sems,
    mg_sems,
    sib_sems,
    halo_sems,
    att_sems,
    rim_sems,
    pr_sems,
    st_sems,
    pk_sems,
):
    rows, width = tokens_ref.shape
    hw = wqkv_hbm.shape[1]
    me = lax.axis_index("dp")
    t = lax.axis_index("tensor")
    px = me + 1 - 2 * lax.rem(me, 2)
    py = me + 2 - 4 * (lax.div(me, 2))
    pd = 3 - me
    sib = t + 1 - 2 * lax.rem(t, 2)
    core = lax.rem(t, 2)
    quarter = rows // 4
    tok_base = t * rows

    barrier = pltpu.get_barrier_semaphore()
    for peer in (px, py, pd):
        pl.semaphore_signal(barrier, inc=1, device_id=(peer, t), device_id_type=MESH)

    @pl.loop(1, nt)
    def _(k):
        pl.semaphore_signal(
            barrier, inc=1, device_id=(me, lax.rem(t + k, nt)), device_id_type=MESH
        )

    tok_copy = pltpu.make_async_copy(tokens_ref, tok.at[0], tok_sem)
    tok_copy.start()
    wq_copy = pltpu.make_async_copy(wqkv_hbm, wqkv_ref, wq_sem)
    wq_copy.start()
    ow_copy = pltpu.make_async_copy(ow_ref, owf.at[0], ow_sem)
    ow_copy.start()
    mw_copy = pltpu.make_async_copy(mw_hbm, mw, mw_sem)
    mw_copy.start()

    pl.semaphore_wait(barrier, 3 + nt - 1)

    def remote(src, dst, send, recv, dev):
        return pltpu.make_async_remote_copy(
            src_ref=src, dst_ref=dst, send_sem=send, recv_sem=recv,
            device_id=dev, device_id_type=MESH,
        )

    def gather_plan(part, sems):
        def cp(src_slot, dst_slot, half, k, dev):
            return remote(
                part(src_slot, half, own=True), part(dst_slot, half),
                sems.at[0, k], sems.at[1, k], (dev, t),
            )
        return {
            "1A": cp(0, 1, 0, 0, px),
            "1B": cp(0, 1, 1, 1, px),
            "2B": cp(0, 2, 1, 2, py),
            "2A": cp(0, 2, 0, 3, py),
            "3A": cp(1, 3, 0, 4, py),
            "3B": cp(2, 3, 1, 5, px),
        }

    def start_own(plan):
        for k in ("1A", "2B", "1B", "2A"):
            plan[k].start()

    def relay(plan):
        plan["1A"].wait_recv()
        plan["3A"].start()
        plan["2B"].wait_recv()
        plan["3B"].start()

    own_ow = hw // 2
    ow_a = (own_ow // 32 + (1 if own_ow % 32 else 0)) * 16
    ow_base = pl.multiple_of(core * own_ow, 16)

    def ow_part(s, h, own=False):
        piece = (
            pl.ds(ow_base, ow_a)
            if h == 0
            else pl.ds(pl.multiple_of(ow_base + ow_a, 16), own_ow - ow_a)
        )
        return ow_ref.at[piece, :] if own and s == 0 else owf.at[s, piece, :]

    owg = gather_plan(ow_part, owg_sems)

    half_rows = rows // 2

    def tok_part(s, h, own=False):
        piece = pl.ds(h * half_rows, half_rows)
        return tokens_ref.at[piece, :] if own and s == 0 else tok.at[s, piece, :]

    ag = gather_plan(tok_part, ag_sems)
    start_own(ag)

    @pl.when(t == 0)
    def _():
        kvx[:, :, 0:SPAN, :] = jnp.zeros((4, 2, SPAN, hw), BF16)
        rim[0:GRID, :] = jnp.zeros((GRID, width), BF16)

    @pl.when(t == nt - 1)
    def _():
        kvx[:, :, SPAN + rows :, :] = jnp.zeros((4, 2, SPAN, hw), BF16)
        rim[GRID + rows :, :] = jnp.zeros((GRID, width), BF16)

    def image_table(group):
        widths = [grids_ref[group, 1, i] for i in range(images)]
        lengths = [grids_ref[group, 0, i] * widths[i] for i in range(images)]
        starts = []
        total = jnp.int32(0)
        for i in range(images):
            starts.append(total)
            total = total + lengths[i]
        return widths, lengths, starts, total

    def lookup(pos, starts, total):
        found = jnp.full(pos.shape, -1, jnp.int32)
        for s in starts:
            found = found + (pos >= s).astype(jnp.int32)
        return jnp.where((pos >= 0) & (pos < total), found, -1)

    def halo(slot, up):
        dev = (me, t + 1) if up else (me, t - 1)
        k = 0 if up else 1
        start = 0 if up else SPAN + rows
        return remote(
            kvx.at[slot, :, pl.ds(SPAN, rows), :],
            kvx.at[slot, :, pl.ds(start, rows), :],
            halo_sems.at[0, k, slot], halo_sems.at[1, k, slot], dev,
        )

    def qkv_step(slot):
        x = tok[slot].astype(F32)
        average = jnp.mean(x, axis=1, keepdims=True)
        centred = x - average
        variance = jnp.mean(centred * centred, axis=1, keepdims=True)
        normed[...] = (
            centred * lax.rsqrt(variance + EPS) * gain_ref[...][None, :] + nbias_ref[...][None, :]
        ).astype(BF16)
        data = normed[...]
        for j in range(3):
            r = (
                lax.dot_general(
                    data, wqkv_ref[j], (((1,), (1,)), ((), ())), preferred_element_type=F32
                )
                + bqkv_ref[j : j + 1, :]
            ).astype(BF16)
            if j == 0:
                queries[slot] = r
            else:
                kvx[slot, j - 1, SPAN : SPAN + rows, :] = r

        @pl.when(t < nt - 1)
        def _():
            halo(slot, True).start()

        @pl.when(t > 0)
        def _():
            halo(slot, False).start()

    def att_copy(slot, b):
        flip = lax.rem(slot, 2)
        high = lax.div(slot, 2)
        peer = me + flip * (1 - 2 * lax.rem(me, 2)) + high * (2 - 4 * lax.div(me, 2))
        return remote(
            att_out.at[slot, pl.ds(b * 128, 128), :], att_in.at[slot, pl.ds(b * 128, 128), :],
            att_sems.at[0, b, slot], att_sems.at[1, b, slot], (peer, t),
        )

    def att_step(slot):
        flip = lax.rem(slot, 2)
        high = lax.div(slot, 2)
        group = me + flip * (1 - 2 * lax.rem(me, 2)) + high * (2 - 4 * lax.div(me, 2))
        _, _, starts, total = image_table(group)
        qpos = tok_base + lax.broadcasted_iota(jnp.int32, (rows, 1), 0)
        kpos = tok_base - SPAN + lax.broadcasted_iota(jnp.int32, (1, rows + 2 * SPAN), 1)
        qimg = lookup(qpos, starts, total)
        kimg = lookup(kpos, starts, total)

        @pl.when(t > 0)
        def _():
            halo(slot, True).wait_recv()

        @pl.when(t < nt - 1)
        def _():
            halo(slot, False).wait_recv()

        blk = 128
        for b in range(rows // blk):
            keys = pl.ds(b * blk, blk + 2 * SPAN)
            kk = kvx[slot, 0, keys, :]
            vv = kvx[slot, 1, keys, :]
            q = queries[slot, b * blk : (b + 1) * blk, :]
            qi = qimg[b * blk : (b + 1) * blk]
            allowed = qi == kimg[:, b * blk : b * blk + blk + 2 * SPAN]
            edges = list(range(0, hw, 128)) + [hw]
            outs = [None] * (len(edges) - 1)
            for h in range(hw // HD):
                first = (h * HD) // 128
                last = ((h + 1) * HD - 1) // 128
                lo, hi = edges[first], edges[last + 1]
                col = lo + lax.broadcasted_iota(jnp.int32, (1, hi - lo), 1)
                mine = (col >= h * HD) & (col < (h + 1) * HD)
                qh = q[:, lo:hi] * jnp.where(mine, 1.0, 0.0).astype(BF16)
                s = lax.dot_general(
                    qh, kk[:, lo:hi], (((1,), (1,)), ((), ())), preferred_element_type=F32
                )
                s = jnp.where(allowed, s, FLOOR)
                w = jnp.exp2((s - jnp.max(s, axis=1, keepdims=True)) * RATE)
                den = jnp.sum(w, axis=1, keepdims=True)
                pv = jnp.dot(w.astype(BF16), vv[:, lo:hi], preferred_element_type=F32)
                pv = pv * jnp.where(qi >= 0, 1.0 / den, 0.0)
                for c in range(first, last + 1):
                    piece = slice(edges[c] - lo, edges[c + 1] - lo)
                    part = pv[:, piece]
                    outs[c] = part if outs[c] is None else jnp.where(mine[:, piece], part, outs[c])
            for c, part in enumerate(outs):
                att_out[slot, b * blk : (b + 1) * blk, edges[c] : edges[c + 1]] = part.astype(BF16)

            @pl.when(slot > 0)
            def _():
                att_copy(slot, b).start()

    @pl.loop(0, 5)
    def _(s):
        @pl.when(s == 0)
        def _():
            tok_copy.wait()
            wq_copy.wait()

        @pl.when(s == 1)
        def _():
            relay(ag)
            owg["1A"].start()
            owg["2B"].start()
            owg["1B"].start()
            owg["2A"].start()
            ag["1B"].wait_recv()

        @pl.when(s == 2)
        def _():
            ag["2A"].wait_recv()

        @pl.when(s == 3)
        def _():
            ag["3A"].wait_recv()
            ag["3B"].wait_recv()

        @pl.when(s < 4)
        def _():
            qkv_step(s)

        @pl.when(s != 1)
        def _():
            att_step(lax.max(s - 1, 0))

    relay(owg)
    owg["1B"].wait_recv()
    owg["2A"].wait_recv()

    def sib_copy(slot):
        part = owf.at[slot, pl.ds(ow_base, own_ow), :]
        return remote(part, part, sib_sems.at[0, slot], sib_sems.at[1, slot], (me, sib))

    sib_copy(1).start()
    sib_copy(2).start()
    ow_copy.wait()
    acc = tok[0].astype(F32) + obias_ref[...][None, :]
    acc = acc + jnp.dot(att_out[0], owf[0], preferred_element_type=F32)
    owg["3A"].wait_recv()
    owg["3B"].wait_recv()
    sib_copy(3).start()
    for slot in (1, 2, 3):
        for b in range(rows // 128):
            att_copy(slot, b).wait_recv()
        sib_copy(slot).wait_recv()
        acc = acc + jnp.dot(att_in[slot], owf[slot], preferred_element_type=F32)
    rim[GRID : GRID + rows, :] = acc.astype(BF16)

    rim_up = remote(
        rim.at[pl.ds(rows, GRID), :], rim.at[pl.ds(0, GRID), :],
        rim_sems.at[0, 0], rim_sems.at[1, 0], (me, t + 1),
    )
    rim_down = remote(
        rim.at[pl.ds(GRID, GRID), :], rim.at[pl.ds(GRID + rows, GRID), :],
        rim_sems.at[0, 1], rim_sems.at[1, 1], (me, t - 1),
    )

    @pl.when(t < nt - 1)
    def _():
        rim_up.start()

    @pl.when(t > 0)
    def _():
        rim_down.start()

    widths, lengths, starts, total = image_table(me)
    lane = lax.broadcasted_iota(jnp.int32, (1, 128), 1)
    qimg = lookup(tok_base + lax.broadcasted_iota(jnp.int32, (rows, 1), 0), starts, total)
    row_sq = jnp.sum(acc * acc, axis=1, keepdims=True)
    squares = jnp.sum(jnp.where(qimg == lane, row_sq, 0.0), axis=0, keepdims=True)

    squares_in[0, 0:1, :] = squares

    def sq_copy(k):
        return remote(
            squares_in.at[0], squares_in.at[k], st_sems.at[0, k], st_sems.at[1, k],
            (me, lax.rem(t + k, nt)),
        )

    @pl.loop(1, nt)
    def _(k):
        sq_copy(k).start()

    def merged_images(group):
        _, _, begins, whole = image_table(group)
        pos = t * quarter + lax.broadcasted_iota(jnp.int32, (quarter, 1), 0)
        return lookup(pos, [lax.div(b, 4) for b in begins], lax.div(whole, 4))

    mpos = t * quarter + lax.broadcasted_iota(jnp.int32, (quarter, 1), 0)
    mimg = lookup(mpos, [lax.div(s, 4) for s in starts], lax.div(total, 4))
    gw = jnp.zeros((quarter, 1), jnp.int32)
    st = jnp.zeros((quarter, 1), jnp.int32)
    for i in range(images):
        hit = mimg == i
        gw = jnp.where(hit, widths[i], gw)
        st = jnp.where(hit, starts[i], st)
    half = lax.shift_right_logical(gw, 1)
    offset = mpos - lax.shift_right_logical(st, 2)
    grow = jnp.zeros((quarter, 1), jnp.int32)
    for r in range(1, GRID // 2):
        grow = grow + (offset >= r * half).astype(jnp.int32)
    anchor = st + 2 * grow * gw + 2 * (offset - grow * half) - (tok_base - GRID)
    valid = mimg >= 0

    @pl.when(t > 0)
    def _():
        rim_up.wait_recv()

    @pl.when(t < nt - 1)
    def _():
        rim_down.wait_recv()

    mg = gather_plan(lambda s, h, own=False: merged.at[s, pl.ds(2 * h, 2), :, :], mg_sems)
    span_iota = lax.broadcasted_iota(jnp.int32, (quarter, rows + 2 * GRID), 1)
    around = rim[...]
    for j, shift in enumerate((0, 1, gw, gw + 1)):
        pick = jnp.where((anchor + shift == span_iota) & valid, 1.0, 0.0).astype(BF16)
        merged[0, j] = jnp.dot(pick, around, preferred_element_type=F32).astype(BF16)
    start_own(mg)
    owners = [mimg, merged_images(px), merged_images(py), merged_images(pd)]
    mw_copy.wait()

    @pl.loop(1, nt)
    def _(k):
        sq_copy(k).wait_recv()

    sq = jnp.sum(squares_in[:, 0, :], axis=0, keepdims=True)
    length = jnp.ones((1, 128), F32)
    for i in range(images):
        length = jnp.where(lane == i, lengths[i].astype(F32), length)
    rms_ref[...] = jnp.sqrt(sq / (length * width))[:, :images]

    def project(slot, halves):
        total = None
        for h in halves:
            for j in (2 * h, 2 * h + 1):
                part = jnp.dot(
                    merged[slot, j], mw[j * width : (j + 1) * width, :],
                    preferred_element_type=F32,
                )
                total = part if total is None else total + part
        return total

    def pr_copy(slot, peer, theirs):
        return remote(
            pr_out.at[slot], pr_in.at[slot],
            pr_sems.at[0, slot], pr_sems.at[1, slot], (peer, t),
        )

    def pk_copy(slot, peer, k):
        return remote(
            peaks_out.at[slot], peaks_in.at[slot, k],
            pk_sems.at[0, slot, k], pk_sems.at[1, slot, k],
            (peer, lax.rem(t + k, nt)),
        )

    peers = (me, px, py, pd)

    def finish(slot):
        block = project(slot, (0, 1)).astype(BF16)
        pr_out[slot] = block
        if slot > 0:
            pr_copy(slot, peers[slot], me).start()
        row_peak = jnp.max(block.astype(F32), axis=1, keepdims=True)
        peaks = jnp.max(jnp.where(owners[slot] == lane, row_peak, FLOOR), axis=0, keepdims=True)
        peaks_out[slot, 0:1, :] = peaks

        @pl.loop(0 if slot > 0 else 1, nt)
        def _(k):
            pk_copy(slot, peers[slot], k).start()

    finish(0)
    relay(mg)
    mg["1B"].wait_recv()
    finish(1)
    mg["2A"].wait_recv()
    finish(2)
    mg["3A"].wait_recv()
    mg["3B"].wait_recv()
    finish(3)

    columns = pr_out.shape[2]
    proj_ref[:, pl.ds(pl.multiple_of(me * columns, 128), columns)] = pr_out[0]
    for slot in (1, 2, 3):
        pr_copy(slot, peers[slot], me).wait_recv()
        proj_ref[:, pl.ds(pl.multiple_of(peers[slot] * columns, 128), columns)] = pr_in[slot]
    pk = peaks_out[0, 0:1, :]
    for slot in range(4):
        @pl.loop(0 if slot > 0 else 1, nt)
        def _(k):
            pk_copy(slot, peers[slot], k).wait_recv()

        head = 0 if slot > 0 else 1
        pk = jnp.maximum(pk, jnp.max(peaks_in[slot, head:, 0, :], axis=0, keepdims=True))
    peak_ref[...] = pk[:, :images]

    for plan in (ag, owg, mg):
        for k in plan:
            plan[k].wait_send()
    for slot in range(4):
        @pl.when(t < nt - 1)
        def _():
            halo(slot, True).wait_send()

        @pl.when(t > 0)
        def _():
            halo(slot, False).wait_send()
    for slot in (1, 2, 3):
        for b in range(rows // 128):
            att_copy(slot, b).wait_send()
        sib_copy(slot).wait_send()
    pr_copy(1, px, me).wait_send()
    pr_copy(2, py, me).wait_send()
    pr_copy(3, pd, me).wait_send()

    @pl.when(t < nt - 1)
    def _():
        rim_up.wait_send()

    @pl.when(t > 0)
    def _():
        rim_down.wait_send()

    @pl.loop(1, nt)
    def _(k):
        sq_copy(k).wait_send()

    for slot in range(4):
        @pl.loop(0 if slot > 0 else 1, nt)
        def _(k):
            pk_copy(slot, peers[slot], k).wait_send()


def hand_over(a, b, c, x, y, z):
    x[...] = a[...]
    y[...] = b[...]
    z[...] = c[...]


def body(nt, tokens, gain, nbias, wqkv, bqkv, ow, obias, mw, grids):
    rows, width = tokens.shape
    hw = wqkv.shape[2]
    images = grids.shape[1]
    columns = mw.shape[1]
    quarter = rows // 4
    vmem = pl.BlockSpec(memory_space=pltpu.VMEM)
    hbm = pl.BlockSpec(memory_space=pl.ANY)
    dma = pltpu.SemaphoreType.DMA
    results = pl.pallas_call(
        functools.partial(kernel, nt, images),
        out_shape=(
            jax.ShapeDtypeStruct((quarter, 4 * columns), BF16),
            jax.ShapeDtypeStruct((1, images), F32),
            jax.ShapeDtypeStruct((1, images), F32),
        ),
        in_specs=[hbm, vmem, vmem, hbm, vmem, hbm, vmem, hbm,
                  pl.BlockSpec(memory_space=pltpu.SMEM)],
        out_specs=(vmem, vmem, vmem),
        scratch_shapes=[
            pltpu.VMEM((4, rows, width), BF16),
            pltpu.VMEM((rows, width), BF16),
            pltpu.VMEM((4, rows, hw), BF16),
            pltpu.VMEM((4, 2, rows + 2 * SPAN, hw), BF16),
            pltpu.VMEM((4, rows, hw), BF16),
            pltpu.VMEM((4, rows, hw), BF16),
            pltpu.VMEM((4, hw, width), BF16),
            pltpu.VMEM((rows + 2 * GRID, width), BF16),
            pltpu.VMEM((4, 4, quarter, width), BF16),
            pltpu.VMEM((4 * width, columns), BF16),
            pltpu.VMEM((4, quarter, columns), BF16),
            pltpu.VMEM((4, quarter, columns), BF16),
            pltpu.VMEM((nt, 8, 128), F32),
            pltpu.VMEM((4, 8, 128), F32),
            pltpu.VMEM((4, nt, 8, 128), F32),
            pltpu.VMEM((3, hw, width), BF16),
            dma,
            dma,
            dma,
            dma,
            dma((2, 6)),
            dma((2, 6)),
            dma((2, 6)),
            dma((2, 4)),
            dma((2, 2, 4)),
            dma((2, rows // 128, 4)),
            dma((2, 2)),
            dma((2, 4)),
            dma((2, nt)),
            dma((2, 4, nt)),
        ],
        compiler_params=pltpu.CompilerParams(
            collective_id=0, has_side_effects=True, vmem_limit_bytes=60 * 1024 * 1024
        ),
        name="vision_block",
    )(
        tokens, gain, nbias, wqkv.transpose(1, 2, 0), bqkv, ow, obias, mw,
        grids.transpose(0, 2, 1),
    )
    return pl.pallas_call(
        hand_over,
        out_shape=tuple(jax.ShapeDtypeStruct(r.shape, r.dtype) for r in results),
        in_specs=[vmem] * 3,
        out_specs=(vmem,) * 3,
        name="hand_over",
    )(*results)


def solution(mesh):
    placed = (
        P(("dp", "tensor"), None),
        P(),
        P(),
        P(None, None, "dp"),
        P(None, "dp"),
        P("dp", None),
        P(),
        P(None, "dp"),
        P(),
    )
    return jax.shard_map(
        functools.partial(body, mesh.shape["tensor"]),
        mesh=mesh,
        in_specs=placed,
        out_specs=(P(("dp", "tensor"), None), P("dp", None), P("dp", None)),
        check_vma=False,
    )
```

```python
import functools
import math

import jax
import jax.numpy as jnp
from jax import lax
from jax.experimental import pallas as pl
from jax.experimental.pallas import tpu as pltpu
from jax.sharding import PartitionSpec as P

HD = 88
GRID = 16
SPAN = GRID * GRID
EPS = 1e-06
FLOOR = -1e30
RATE = 1.0 / (math.sqrt(HD) * math.log(2.0))
MESH = pl.DeviceIdType.MESH
F32 = jnp.float32
BF16 = jnp.bfloat16


def kernel(
    nt,
    images,
    tokens_ref,
    gain_ref,
    nbias_ref,
    wqkv_hbm,
    bqkv_ref,
    ow_ref,
    obias_ref,
    mw_hbm,
    grids_ref,
    proj_ref,
    rms_ref,
    peak_ref,
    tok,
    normed,
    queries,
    kvx,
    att_out,
    att_in,
    owf,
    rim,
    merged,
    mw,
    pr_out,
    pr_in,
    squares_in,
    peaks_out,
    peaks_in,
    wqkv_ref,
    tok_sem,
    wq_sem,
    mw_sem,
    ow_sem,
    ag_sems,
    owg_sems,
    mg_sems,
    sib_sems,
    halo_sems,
    att_sems,
    rim_sems,
    pr_sems,
    st_sems,
    pk_sems,
):
    rows, width = tokens_ref.shape
    hw = wqkv_hbm.shape[1]
    me = lax.axis_index("dp")
    t = lax.axis_index("tensor")
    px = me + 1 - 2 * lax.rem(me, 2)
    py = me + 2 - 4 * (lax.div(me, 2))
    pd = 3 - me
    sib = t + 1 - 2 * lax.rem(t, 2)
    core = lax.rem(t, 2)
    quarter = rows // 4
    tok_base = t * rows

    barrier = pltpu.get_barrier_semaphore()
    for peer in (px, py, pd):
        pl.semaphore_signal(barrier, inc=1, device_id=(peer, t), device_id_type=MESH)

    @pl.loop(1, nt)
    def _(k):
        pl.semaphore_signal(
            barrier, inc=1, device_id=(me, lax.rem(t + k, nt)), device_id_type=MESH
        )

    tok_copy = pltpu.make_async_copy(tokens_ref, tok.at[0], tok_sem)
    tok_copy.start()
    wq_copy = pltpu.make_async_copy(wqkv_hbm, wqkv_ref, wq_sem)
    wq_copy.start()
    ow_copy = pltpu.make_async_copy(ow_ref, owf.at[0], ow_sem)
    ow_copy.start()
    mw_copy = pltpu.make_async_copy(mw_hbm, mw, mw_sem)
    mw_copy.start()

    pl.semaphore_wait(barrier, 3 + nt - 1)

    def remote(src, dst, send, recv, dev):
        return pltpu.make_async_remote_copy(
            src_ref=src, dst_ref=dst, send_sem=send, recv_sem=recv,
            device_id=dev, device_id_type=MESH,
        )

    def gather_plan(part, sems):
        def cp(src_slot, dst_slot, half, k, dev):
            return remote(
                part(src_slot, half, own=True), part(dst_slot, half),
                sems.at[0, k], sems.at[1, k], (dev, t),
            )
        return {
            "1A": cp(0, 1, 0, 0, px),
            "1B": cp(0, 1, 1, 1, px),
            "2B": cp(0, 2, 1, 2, py),
            "2A": cp(0, 2, 0, 3, py),
            "3A": cp(1, 3, 0, 4, py),
            "3B": cp(2, 3, 1, 5, px),
        }

    def start_own(plan):
        for k in ("1A", "2B", "1B", "2A"):
            plan[k].start()

    def relay(plan):
        plan["1A"].wait_recv()
        plan["3A"].start()
        plan["2B"].wait_recv()
        plan["3B"].start()

    own_ow = hw // 2
    ow_a = (own_ow // 32 + (1 if own_ow % 32 else 0)) * 16
    ow_base = pl.multiple_of(core * own_ow, 16)

    def ow_part(s, h, own=False):
        piece = (
            pl.ds(ow_base, ow_a)
            if h == 0
            else pl.ds(pl.multiple_of(ow_base + ow_a, 16), own_ow - ow_a)
        )
        return ow_ref.at[piece, :] if own and s == 0 else owf.at[s, piece, :]

    owg = gather_plan(ow_part, owg_sems)

    half_rows = rows // 2

    def tok_part(s, h, own=False):
        piece = pl.ds(h * half_rows, half_rows)
        return tokens_ref.at[piece, :] if own and s == 0 else tok.at[s, piece, :]

    ag = gather_plan(tok_part, ag_sems)
    ag["1A"].start()
    ag["2B"].start()
    owg["1A"].start()
    owg["2B"].start()
    ag["1B"].start()
    ag["2A"].start()

    @pl.when(t == 0)
    def _():
        kvx[:, :, 0:SPAN, :] = jnp.zeros((4, 2, SPAN, hw), BF16)
        rim[0:GRID, :] = jnp.zeros((GRID, width), BF16)

    @pl.when(t == nt - 1)
    def _():
        kvx[:, :, SPAN + rows :, :] = jnp.zeros((4, 2, SPAN, hw), BF16)
        rim[GRID + rows :, :] = jnp.zeros((GRID, width), BF16)

    def image_table(group):
        widths = [grids_ref[group, 1, i] for i in range(images)]
        lengths = [grids_ref[group, 0, i] * widths[i] for i in range(images)]
        starts = []
        total = jnp.int32(0)
        for i in range(images):
            starts.append(total)
            total = total + lengths[i]
        return widths, lengths, starts, total

    def lookup(pos, starts, total):
        found = jnp.full(pos.shape, -1, jnp.int32)
        for s in starts:
            found = found + (pos >= s).astype(jnp.int32)
        return jnp.where((pos >= 0) & (pos < total), found, -1)

    def halo(slot, up):
        dev = (me, t + 1) if up else (me, t - 1)
        k = 0 if up else 1
        start = 0 if up else SPAN + rows
        return remote(
            kvx.at[slot, :, pl.ds(SPAN, rows), :],
            kvx.at[slot, :, pl.ds(start, rows), :],
            halo_sems.at[0, k, slot], halo_sems.at[1, k, slot], dev,
        )

    def qkv_step(slot):
        x = tok[slot].astype(F32)
        average = jnp.mean(x, axis=1, keepdims=True)
        centred = x - average
        variance = jnp.mean(centred * centred, axis=1, keepdims=True)
        normed[...] = (
            centred * lax.rsqrt(variance + EPS) * gain_ref[...][None, :] + nbias_ref[...][None, :]
        ).astype(BF16)
        data = normed[...]
        for j in range(3):
            r = (
                lax.dot_general(
                    data, wqkv_ref[j], (((1,), (1,)), ((), ())), preferred_element_type=F32
                )
                + bqkv_ref[j : j + 1, :]
            ).astype(BF16)
            if j == 0:
                queries[slot] = r
            else:
                kvx[slot, j - 1, SPAN : SPAN + rows, :] = r

        @pl.when(t < nt - 1)
        def _():
            halo(slot, True).start()

        @pl.when(t > 0)
        def _():
            halo(slot, False).start()

    def att_copy(slot, b):
        flip = lax.rem(slot, 2)
        high = lax.div(slot, 2)
        peer = me + flip * (1 - 2 * lax.rem(me, 2)) + high * (2 - 4 * lax.div(me, 2))
        return remote(
            att_out.at[slot, pl.ds(b * 128, 128), :], att_in.at[slot, pl.ds(b * 128, 128), :],
            att_sems.at[0, b, slot], att_sems.at[1, b, slot], (peer, t),
        )

    def att_step(slot):
        flip = lax.rem(slot, 2)
        high = lax.div(slot, 2)
        group = me + flip * (1 - 2 * lax.rem(me, 2)) + high * (2 - 4 * lax.div(me, 2))
        _, _, starts, total = image_table(group)
        qpos = tok_base + lax.broadcasted_iota(jnp.int32, (rows, 1), 0)
        kpos = tok_base - SPAN + lax.broadcasted_iota(jnp.int32, (1, rows + 2 * SPAN), 1)
        qimg = lookup(qpos, starts, total)
        kimg = lookup(kpos, starts, total)

        @pl.when(t > 0)
        def _():
            halo(slot, True).wait_recv()

        @pl.when(t < nt - 1)
        def _():
            halo(slot, False).wait_recv()

        blk = 128
        for b in range(rows // blk):
            keys = pl.ds(b * blk, blk + 2 * SPAN)
            kk = kvx[slot, 0, keys, :]
            vv = kvx[slot, 1, keys, :]
            q = queries[slot, b * blk : (b + 1) * blk, :]
            qi = qimg[b * blk : (b + 1) * blk]
            allowed = qi == kimg[:, b * blk : b * blk + blk + 2 * SPAN]
            edges = list(range(0, hw, 128)) + [hw]
            outs = [None] * (len(edges) - 1)
            for h in range(hw // HD):
                first = (h * HD) // 128
                last = ((h + 1) * HD - 1) // 128
                lo, hi = edges[first], edges[last + 1]
                col = lo + lax.broadcasted_iota(jnp.int32, (1, hi - lo), 1)
                mine = (col >= h * HD) & (col < (h + 1) * HD)
                qh = q[:, lo:hi] * jnp.where(mine, 1.0, 0.0).astype(BF16)
                s = lax.dot_general(
                    qh, kk[:, lo:hi], (((1,), (1,)), ((), ())), preferred_element_type=F32
                )
                s = jnp.where(allowed, s, FLOOR)
                w = jnp.exp2((s - jnp.max(s, axis=1, keepdims=True)) * RATE)
                den = jnp.sum(w, axis=1, keepdims=True)
                pv = jnp.dot(w.astype(BF16), vv[:, lo:hi], preferred_element_type=F32)
                pv = pv * jnp.where(qi >= 0, 1.0 / den, 0.0)
                for c in range(first, last + 1):
                    piece = slice(edges[c] - lo, edges[c + 1] - lo)
                    part = pv[:, piece]
                    outs[c] = part if outs[c] is None else jnp.where(mine[:, piece], part, outs[c])
            for c, part in enumerate(outs):
                att_out[slot, b * blk : (b + 1) * blk, edges[c] : edges[c + 1]] = part.astype(BF16)

            @pl.when(slot > 0)
            def _():
                att_copy(slot, b).start()

    @pl.loop(0, 5)
    def _(s):
        @pl.when(s == 0)
        def _():
            tok_copy.wait()
            wq_copy.wait()

        @pl.when(s == 1)
        def _():
            relay(ag)
            ag["1B"].wait_recv()

        @pl.when(s == 2)
        def _():
            ag["2A"].wait_recv()
            relay(owg)
            owg["1B"].start()
            owg["2A"].start()

        @pl.when(s == 3)
        def _():
            ag["3A"].wait_recv()
            ag["3B"].wait_recv()

        @pl.when(s < 4)
        def _():
            qkv_step(s)

        @pl.when(s != 1)
        def _():
            att_step(lax.max(s - 1, 0))

    owg["1B"].wait_recv()
    owg["2A"].wait_recv()

    def sib_copy(slot):
        part = owf.at[slot, pl.ds(ow_base, own_ow), :]
        return remote(part, part, sib_sems.at[0, slot], sib_sems.at[1, slot], (me, sib))

    sib_copy(1).start()
    sib_copy(2).start()
    ow_copy.wait()
    acc = tok[0].astype(F32) + obias_ref[...][None, :]
    acc = acc + jnp.dot(att_out[0], owf[0], preferred_element_type=F32)
    owg["3A"].wait_recv()
    owg["3B"].wait_recv()
    sib_copy(3).start()
    for slot in (1, 2, 3):
        for b in range(rows // 128):
            att_copy(slot, b).wait_recv()
        sib_copy(slot).wait_recv()
        acc = acc + jnp.dot(att_in[slot], owf[slot], preferred_element_type=F32)
    rim[GRID : GRID + rows, :] = acc.astype(BF16)

    rim_up = remote(
        rim.at[pl.ds(rows, GRID), :], rim.at[pl.ds(0, GRID), :],
        rim_sems.at[0, 0], rim_sems.at[1, 0], (me, t + 1),
    )
    rim_down = remote(
        rim.at[pl.ds(GRID, GRID), :], rim.at[pl.ds(GRID + rows, GRID), :],
        rim_sems.at[0, 1], rim_sems.at[1, 1], (me, t - 1),
    )

    @pl.when(t < nt - 1)
    def _():
        rim_up.start()

    @pl.when(t > 0)
    def _():
        rim_down.start()

    widths, lengths, starts, total = image_table(me)
    lane = lax.broadcasted_iota(jnp.int32, (1, 128), 1)
    qimg = lookup(tok_base + lax.broadcasted_iota(jnp.int32, (rows, 1), 0), starts, total)
    row_sq = jnp.sum(acc * acc, axis=1, keepdims=True)
    squares = jnp.sum(jnp.where(qimg == lane, row_sq, 0.0), axis=0, keepdims=True)

    squares_in[0] = squares

    def sq_copy(k):
        return remote(
            squares_in.at[0], squares_in.at[k], st_sems.at[0, k], st_sems.at[1, k],
            (me, lax.rem(t + k, nt)),
        )

    @pl.loop(1, nt)
    def _(k):
        sq_copy(k).start()

    def merged_images(group):
        _, _, begins, whole = image_table(group)
        pos = t * quarter + lax.broadcasted_iota(jnp.int32, (quarter, 1), 0)
        return lookup(pos, [lax.div(b, 4) for b in begins], lax.div(whole, 4))

    mpos = t * quarter + lax.broadcasted_iota(jnp.int32, (quarter, 1), 0)
    mimg = lookup(mpos, [lax.div(s, 4) for s in starts], lax.div(total, 4))
    gw = jnp.zeros((quarter, 1), jnp.int32)
    st = jnp.zeros((quarter, 1), jnp.int32)
    for i in range(images):
        hit = mimg == i
        gw = jnp.where(hit, widths[i], gw)
        st = jnp.where(hit, starts[i], st)
    half = lax.shift_right_logical(gw, 1)
    offset = mpos - lax.shift_right_logical(st, 2)
    grow = jnp.zeros((quarter, 1), jnp.int32)
    for r in range(1, GRID // 2):
        grow = grow + (offset >= r * half).astype(jnp.int32)
    anchor = st + 2 * grow * gw + 2 * (offset - grow * half) - (tok_base - GRID)
    valid = mimg >= 0

    @pl.when(t > 0)
    def _():
        rim_up.wait_recv()

    @pl.when(t < nt - 1)
    def _():
        rim_down.wait_recv()

    mg = gather_plan(lambda s, h, own=False: merged.at[s, pl.ds(2 * h, 2), :, :], mg_sems)
    span_iota = lax.broadcasted_iota(jnp.int32, (quarter, rows + 2 * GRID), 1)
    around = rim[...]
    for j, shift in enumerate((0, 1, gw, gw + 1)):
        pick = jnp.where((anchor + shift == span_iota) & valid, 1.0, 0.0).astype(BF16)
        merged[0, j] = jnp.dot(pick, around, preferred_element_type=F32).astype(BF16)
    start_own(mg)
    owners = [mimg, merged_images(px), merged_images(py), merged_images(pd)]
    mw_copy.wait()

    @pl.loop(1, nt)
    def _(k):
        sq_copy(k).wait_recv()

    sq = jnp.sum(squares_in[...], axis=0)
    length = jnp.ones((1, 128), F32)
    for i in range(images):
        length = jnp.where(lane == i, lengths[i].astype(F32), length)
    rms_ref[...] = jnp.sqrt(sq / (length * width))[:, :images]

    def project(slot, halves):
        total = None
        for h in halves:
            for j in (2 * h, 2 * h + 1):
                part = jnp.dot(
                    merged[slot, j], mw[j * width : (j + 1) * width, :],
                    preferred_element_type=F32,
                )
                total = part if total is None else total + part
        return total

    def pr_copy(slot, peer, theirs):
        return remote(
            pr_out.at[slot], pr_in.at[slot],
            pr_sems.at[0, slot], pr_sems.at[1, slot], (peer, t),
        )

    def pk_copy(slot, peer, k):
        return remote(
            peaks_out.at[slot], peaks_in.at[slot, k],
            pk_sems.at[0, slot, k], pk_sems.at[1, slot, k],
            (peer, lax.rem(t + k, nt)),
        )

    peers = (me, px, py, pd)

    def finish(slot):
        block = project(slot, (0, 1)).astype(BF16)
        pr_out[slot] = block
        row_peak = jnp.max(block.astype(F32), axis=1, keepdims=True)
        peaks = jnp.max(jnp.where(owners[slot] == lane, row_peak, FLOOR), axis=0, keepdims=True)
        peaks_out[slot] = peaks

        @pl.loop(0 if slot > 0 else 1, nt)
        def _(k):
            pk_copy(slot, peers[slot], k).start()

        if slot > 0:
            pr_copy(slot, peers[slot], me).start()

    finish(0)
    relay(mg)
    mg["1B"].wait_recv()
    finish(1)
    mg["2A"].wait_recv()
    finish(2)
    mg["3A"].wait_recv()
    mg["3B"].wait_recv()
    finish(3)

    columns = pr_out.shape[2]
    proj_ref[:, pl.ds(pl.multiple_of(me * columns, 128), columns)] = pr_out[0]
    for slot in (1, 2, 3):
        pr_copy(slot, peers[slot], me).wait_recv()
        proj_ref[:, pl.ds(pl.multiple_of(peers[slot] * columns, 128), columns)] = pr_in[slot]
    pk = peaks_out[0]
    for slot in range(4):
        @pl.loop(0 if slot > 0 else 1, nt)
        def _(k):
            pk_copy(slot, peers[slot], k).wait_recv()

        head = 0 if slot > 0 else 1
        pk = jnp.maximum(pk, jnp.max(peaks_in[slot, head:], axis=0))
    peak_ref[...] = pk[:, :images]

    for plan in (ag, owg, mg):
        for k in plan:
            plan[k].wait_send()
    for slot in range(4):
        @pl.when(t < nt - 1)
        def _():
            halo(slot, True).wait_send()

        @pl.when(t > 0)
        def _():
            halo(slot, False).wait_send()
    for slot in (1, 2, 3):
        for b in range(rows // 128):
            att_copy(slot, b).wait_send()
        sib_copy(slot).wait_send()
    pr_copy(1, px, me).wait_send()
    pr_copy(2, py, me).wait_send()
    pr_copy(3, pd, me).wait_send()

    @pl.when(t < nt - 1)
    def _():
        rim_up.wait_send()

    @pl.when(t > 0)
    def _():
        rim_down.wait_send()

    @pl.loop(1, nt)
    def _(k):
        sq_copy(k).wait_send()

    for slot in range(4):
        @pl.loop(0 if slot > 0 else 1, nt)
        def _(k):
            pk_copy(slot, peers[slot], k).wait_send()


def hand_over(a, b, c, x, y, z):
    x[...] = a[...]
    y[...] = b[...]
    z[...] = c[...]


def body(nt, tokens, gain, nbias, wqkv, bqkv, ow, obias, mw, grids):
    rows, width = tokens.shape
    hw = wqkv.shape[2]
    images = grids.shape[1]
    columns = mw.shape[1]
    quarter = rows // 4
    vmem = pl.BlockSpec(memory_space=pltpu.VMEM)
    hbm = pl.BlockSpec(memory_space=pl.ANY)
    dma = pltpu.SemaphoreType.DMA
    results = pl.pallas_call(
        functools.partial(kernel, nt, images),
        out_shape=(
            jax.ShapeDtypeStruct((quarter, 4 * columns), BF16),
            jax.ShapeDtypeStruct((1, images), F32),
            jax.ShapeDtypeStruct((1, images), F32),
        ),
        in_specs=[hbm, vmem, vmem, hbm, vmem, hbm, vmem, hbm,
                  pl.BlockSpec(memory_space=pltpu.SMEM)],
        out_specs=(vmem, vmem, vmem),
        scratch_shapes=[
            pltpu.VMEM((4, rows, width), BF16),
            pltpu.VMEM((rows, width), BF16),
            pltpu.VMEM((4, rows, hw), BF16),
            pltpu.VMEM((4, 2, rows + 2 * SPAN, hw), BF16),
            pltpu.VMEM((4, rows, hw), BF16),
            pltpu.VMEM((4, rows, hw), BF16),
            pltpu.VMEM((4, hw, width), BF16),
            pltpu.VMEM((rows + 2 * GRID, width), BF16),
            pltpu.VMEM((4, 4, quarter, width), BF16),
            pltpu.VMEM((4 * width, columns), BF16),
            pltpu.VMEM((4, quarter, columns), BF16),
            pltpu.VMEM((4, quarter, columns), BF16),
            pltpu.VMEM((nt, 1, 128), F32),
            pltpu.VMEM((4, 1, 128), F32),
            pltpu.VMEM((4, nt, 1, 128), F32),
            pltpu.VMEM((3, hw, width), BF16),
            dma,
            dma,
            dma,
            dma,
            dma((2, 6)),
            dma((2, 6)),
            dma((2, 6)),
            dma((2, 4)),
            dma((2, 2, 4)),
            dma((2, rows // 128, 4)),
            dma((2, 2)),
            dma((2, 4)),
            dma((2, nt)),
            dma((2, 4, nt)),
        ],
        compiler_params=pltpu.CompilerParams(
            collective_id=0, has_side_effects=True, vmem_limit_bytes=60 * 1024 * 1024
        ),
        name="vision_block",
    )(
        tokens, gain, nbias, wqkv.transpose(1, 2, 0), bqkv, ow, obias, mw,
        grids.transpose(0, 2, 1),
    )
    return pl.pallas_call(
        hand_over,
        out_shape=tuple(jax.ShapeDtypeStruct(r.shape, r.dtype) for r in results),
        in_specs=[vmem] * 3,
        out_specs=(vmem,) * 3,
        name="hand_over",
    )(*results)


def solution(mesh):
    placed = (
        P(("dp", "tensor"), None),
        P(),
        P(),
        P(None, None, "dp"),
        P(None, "dp"),
        P("dp", None),
        P(),
        P(None, "dp"),
        P(),
    )
    return jax.shard_map(
        functools.partial(body, mesh.shape["tensor"]),
        mesh=mesh,
        in_specs=placed,
        out_specs=(P(("dp", "tensor"), None), P("dp", None), P("dp", None)),
        check_vma=False,
    )
```
